512 devices in a mesh: seq: 16 (over x, y), chan: 32 (over z, core).
Axes of the slice: x: 4, y: 4, z: 16, core: 2. Of those that a mesh axis runs over, the one named last changes fastest.
Arguments:
- grad_out: bfloat16 [8192, 4096], P('seq', 'chan'), may hold values from -6 to 6
- activation: bfloat16 [8192, 4096], P('seq', 'chan'), may hold values from -6 to 6
- residues: float32 [4096, 16], P('chan'), may hold values from -1.5 to 1.5
- decay: float32 [4096, 16], P('chan'), may hold values from 2.4414063e-05 to 0.0333333333
- skip: float32 [4096], P('chan'), may hold values from -3 to 3
- in_weight: bfloat16 [4096, 4096], P('chan'), may hold values from -0.09375 to 0.09375
Outputs:
- input_grad: bfloat16 [8192, 4096], P('seq', 'chan')
- residue_grad: float32 [4096, 16], P('chan')
The draws below stay inside these ranges and needn't reach their ends.
All inputs are finite; a program needn't handle non-finite values.
Results may differ from the reference program's by a relative error of at most 0.012.
Values may be sent and summed in bfloat16 or wider, within the bound.
A program may use at most 64 MiB of HBM per device.

```python
import math
import jax
import jax.numpy as jnp
from jax import lax

D = 4096
ORDER = 16
SEQ_LEN = 8192


def draw_decay(key, part):
    key_pick, key_slow, key_fast = jax.random.split(key, 3)
    shape = (D, ORDER)
    slow_share = 0.5
    picker = jax.random.uniform(key_pick, shape, jnp.float32)
    slow = jnp.exp(jax.random.uniform(key_slow, shape, jnp.float32, math.log(0.2 / SEQ_LEN), math.log(2.0 / SEQ_LEN)))
    fast = jnp.exp(jax.random.uniform(key_fast, shape, jnp.float32, math.log(1.0 / 50.0), math.log(1.0 / 30.0)))
    return jnp.where(picker < slow_share, slow, fast).astype(jnp.float32)


def steps_of(own_key, dims, cuts, least, high):
    loudness = 1.0
    for position, parts in cuts:
        steps = jax.random.uniform(jax.random.fold_in(jax.random.fold_in(own_key, 6), position), (parts,), jnp.float32, least / len(cuts), high / len(cuts))
        loudness = loudness * jnp.repeat(jnp.exp(steps), dims[position] // parts).reshape((-1,) + (1,) * (len(dims) - 1 - position))
    return loudness


def gaussian(rng, dims, deviation, most, cuts=(), held_as=jnp.bfloat16):
    array = jax.random.normal(rng, dims, jnp.float32) * deviation
    if len(cuts) > 0:
        array = steps_of(rng, dims, cuts, -0.22, 0.18) * array
    return jnp.clip(array, min=-most, max=most).astype(held_as)


def setup_inputs(seed: int = 0) -> dict:
    keys = jax.random.split(jax.random.key(seed), 7)
    return {
        "grad_out": gaussian(keys[0], (SEQ_LEN, D), 1.0, 6.0, ((0, 16), (1, 32))),
        "activation": gaussian(keys[1], (SEQ_LEN, D), 1.0, 6.0, ((0, 16), (1, 32))),
        "residues": gaussian(keys[2], (D, ORDER), ORDER ** -0.5, 1.5, ((0, 32),), jnp.float32),
        "decay": draw_decay(jax.random.fold_in(keys[6], 71), 0),
        "skip": gaussian(keys[4], (D,), 1.0, 3.0, ((0, 32),), jnp.float32),
        "in_weight": gaussian(keys[5], (D, D), D ** -0.5, 0.09375, ((0, 32),)),
    }


def reference(grad_out, activation, residues, decay, skip, in_weight):
    length = SEQ_LEN
    upstream = grad_out.astype(jnp.float32)
    source = activation.astype(jnp.float32)
    scale = jnp.sqrt(2.0 * decay)
    times = jnp.arange(length).astype(jnp.float32)
    filter_time = jnp.zeros((length, D), jnp.float32)
    for index in range(ORDER):
        strength = residues[:, index] * scale[:, index]
        filter_time = filter_time + strength[None, :] * jnp.exp(-decay[:, index][None, :] * times[:, None])
    upstream_spec = jnp.fft.rfft(upstream, n=2 * length, axis=0)
    filter_spec = jnp.fft.rfft(filter_time, n=2 * length, axis=0)
    source_spec = jnp.fft.rfft(source, n=2 * length, axis=0)
    conv_time = jnp.fft.irfft(upstream_spec * jnp.conj(filter_spec), n=2 * length, axis=0)[:length]
    conv_grad = (conv_time + skip[None, :] * upstream).astype(jnp.bfloat16)
    filt_grad = jnp.fft.irfft(upstream_spec * jnp.conj(source_spec), n=2 * length, axis=0)[:length]
    columns = []
    for index in range(ORDER):
        weighted = filt_grad * jnp.exp(-decay[:, index][None, :] * times[:, None])
        columns.append(lax.optimization_barrier(jnp.sum(weighted, axis=0)) * scale[:, index])
    residue_grad = jnp.stack(columns, axis=1) / jnp.sqrt(jnp.float32(length))
    input_grad = jnp.dot(conv_grad, in_weight.T, preferred_element_type=jnp.float32).astype(jnp.bfloat16)
    return (input_grad, residue_grad)
```

```python
import functools
import math

import jax
import jax.numpy as jnp
from jax import lax
from jax.experimental import pallas as pl
from jax.experimental.pallas import tpu as pltpu
from jax.sharding import PartitionSpec as P

MESH = pl.DeviceIdType.MESH
SUB = 8
PIECES = 4


def kernel(
    nseq,
    nz,
    scale_len,
    g_hbm,
    act_hbm,
    res_hbm,
    dec_hbm,
    skip_hbm,
    w_hbm,
    out_ref,
    rg_ref,
    gath,
    w_v,
    g_b,
    act_b,
    res_v,
    dec_v,
    skip_v,
    g_f,
    act_f,
    y_f,
    acc,
    nat,
    a_bc,
    r_bc,
    z_bc,
    l_bc,
    b_bc,
    c_bc,
    dec_t,
    states,
    parts,
    load_sem,
    st_send,
    st_recv,
    pt_send,
    pt_recv,
    up_send,
    up_recv,
    dn_send,
    dn_recv,
    pr_send,
    pr_recv,
):
    rows, lanes = g_b.shape
    orders = dec_v.shape[1]
    steps = rows // SUB
    half = nz // 2
    piece = rows // PIECES
    me_s = lax.axis_index("seq")
    me_c = lax.axis_index("chan")
    me_z = me_c // 2
    core = me_c % 2
    partner = me_z * 2 + (1 - core)
    above = ((me_z + 1) % nz) * 2 + core
    below = ((me_z + nz - 1) % nz) * 2 + core

    def load(src, dst, index):
        return pltpu.make_async_copy(src, dst, load_sem.at[index])

    loads = [
        load(g_hbm, g_b, 0),
        load(dec_hbm, dec_v, 1),
        load(res_hbm, res_v, 2),
        load(skip_hbm, skip_v, 3),
        load(act_hbm, act_b, 4),
        load(w_hbm, w_v, 5),
    ]
    barrier = pltpu.get_barrier_semaphore()
    for hop in range(1, nseq):
        pl.semaphore_signal(
            barrier, inc=1, device_id=((me_s + hop) % nseq, me_c), device_id_type=MESH
        )
    for other in (partner, above, below):
        pl.semaphore_signal(barrier, inc=1, device_id=(me_s, other), device_id_type=MESH)
    for copy in loads:
        copy.start()

    loads[1].wait()
    loads[2].wait()
    loads[3].wait()
    decay_t = jnp.transpose(dec_v[...])
    dec_t[...] = decay_t
    weight_t = jnp.sqrt(2.0 * decay_t)
    strength_t = jnp.transpose(res_v[...]) * weight_t
    pole_t = jnp.exp(-decay_t)
    for n in range(orders):
        a_bc[n] = jnp.broadcast_to(pole_t[n : n + 1], (SUB, lanes))
        r_bc[n] = jnp.broadcast_to(strength_t[n : n + 1], (SUB, lanes))
    acc[...] = jnp.zeros_like(acc)

    loads[0].wait()
    loads[4].wait()
    g_f[...] = g_b[...].astype(jnp.float32)
    act_f[...] = act_b[...].astype(jnp.float32)

    zero = jnp.zeros((SUB, lanes), jnp.float32)
    skip_row = jnp.broadcast_to(skip_v[...], (SUB, lanes))
    group = orders // 2
    unroll = 2
    for part in range(2):
        chosen = range(part * group, (part + 1) * group)
        poles = [a_bc[n] for n in chosen]
        gains = [r_bc[n] for n in chosen]

        def scan(index, carry, poles=poles, gains=gains, part=part):
            state, total = list(carry[0]), list(carry[1])
            for inner in range(unroll):
                k = index * unroll + inner
                g_row = g_f[pl.ds(steps - 1 - k, SUB, stride=steps), :]
                act_row = act_f[pl.ds(steps - 1 - k, SUB, stride=steps), :]
                where = pl.ds(pl.multiple_of(k * SUB, SUB), SUB)
                y = skip_row * g_row if part == 0 else y_f[where, :]
                terms = []
                for m in range(group):
                    state[m] = g_row + poles[m] * state[m]
                    terms.append(gains[m] * state[m])
                    total[m] = total[m] + act_row * state[m]
                while len(terms) > 1:
                    terms = [terms[i] + terms[i + 1] for i in range(0, len(terms), 2)]
                y_f[where, :] = y + terms[0]
            return tuple(state), tuple(total)

        state, total = lax.fori_loop(
            0, steps // unroll, scan, ((zero,) * group, (zero,) * group)
        )
        for m, n in enumerate(chosen):
            z_bc[n] = state[m]
            l_bc[n] = total[m]

    row = lax.broadcasted_iota(jnp.int32, (SUB, lanes), 0)
    for n in range(orders):
        rate = jnp.broadcast_to(dec_t[n : n + 1, :], (SUB, lanes))
        state = z_bc[n]
        shift = 1
        while shift < SUB:
            moved = jnp.where(row < SUB - shift, pltpu.roll(state, SUB - shift, 0), 0.0)
            state = state + jnp.exp(rate * float(-steps * shift)) * moved
            shift *= 2
        states[me_s, n : n + 1, :] = state[0:1]
        z_bc[n] = jnp.where(row < SUB - 1, pltpu.roll(state, SUB - 1, 0), 0.0)

    pl.semaphore_wait(barrier, nseq - 1 + 3)

    def to_peer(buffer, send, recv, hop):
        peer = (me_s + hop) % nseq
        return pltpu.make_async_remote_copy(
            src_ref=buffer.at[me_s],
            dst_ref=buffer.at[me_s],
            send_sem=send.at[hop],
            recv_sem=recv.at[me_s],
            device_id=(peer, me_c),
            device_id_type=MESH,
        )

    def from_peer(buffer, send, recv, hop):
        peer = (me_s + hop) % nseq
        return pltpu.make_async_remote_copy(
            src_ref=buffer.at[peer],
            dst_ref=buffer.at[peer],
            send_sem=send.at[hop],
            recv_sem=recv.at[peer],
            device_id=(peer, me_c),
            device_id_type=MESH,
        )

    for hop in range(1, nseq):
        to_peer(states, st_send, st_recv, hop).start()

    def weigh(index, carry):
        carry = list(carry)
        for inner in range(unroll):
            j = index * unroll + inner
            act_row = act_f[pl.ds(j, SUB, stride=steps), :]
            for n in range(orders):
                carry[n] = a_bc[n] * (carry[n] + act_row)
        return tuple(carry)

    weights = lax.fori_loop(0, steps // unroll, weigh, (zero,) * orders)
    distance = (SUB - 1 - row).astype(jnp.float32) * float(steps)
    for n in range(orders):
        b_bc[n] = weights[n]
        rate = jnp.broadcast_to(dec_t[n : n + 1, :], (SUB, lanes))
        c_bc[n] = jnp.exp(-rate * distance)
    block_pole = jnp.exp(dec_t[...] * float(-rows))

    for hop in range(1, nseq):
        from_peer(states, st_send, st_recv, hop).wait_recv()
    enter = jnp.zeros((orders, lanes), jnp.float32)
    for later in range(nseq - 1, 0, -1):
        enter = jnp.where(later > me_s, states[later] + block_pole * enter, enter)
    for n in range(orders):
        c_bc[n] = z_bc[n] + c_bc[n] * jnp.broadcast_to(enter[n : n + 1], (SUB, lanes))

    def rows_of(p):
        return pl.ds(pl.multiple_of(p * piece, piece), piece)

    def ring(slot, s, p, send, recv, to):
        view = gath.at[slot, rows_of(p), :]
        return pltpu.make_async_remote_copy(
            src_ref=view,
            dst_ref=view,
            send_sem=send.at[s, p],
            recv_sem=recv.at[s, p],
            device_id=(me_s, to),
            device_id_type=MESH,
        )

    def go_up(slot, s, p):
        return ring(slot, s, p, up_send, up_recv, above)

    def go_dn(slot, s, p):
        return ring(slot, s, p, dn_send, dn_recv, below)

    def across(slot, d, s, p):
        view = gath.at[slot, rows_of(p), :]
        return pltpu.make_async_remote_copy(
            src_ref=view,
            dst_ref=view,
            send_sem=pr_send.at[d, s, p],
            recv_sem=pr_recv.at[d, s, p],
            device_id=(me_s, partner),
            device_id_type=MESH,
        )

    def chip_up(s):
        return (me_z + nz - s) % nz

    def chip_dn(s):
        return (me_z + s) % nz

    poles = [a_bc[n] for n in range(orders)]
    entering = tuple(r_bc[n] * c_bc[n] for n in range(orders))

    def finish(p, carry):
        def pair(index, carry):
            ys = []
            for inner in range(2):
                k = p * (piece // SUB) + index * 2 + inner
                carry = [poles[n] * carry[n] for n in range(orders)]
                terms = list(carry)
                while len(terms) > 1:
                    terms = [terms[i] + terms[i + 1] for i in range(0, len(terms), 2)]
                ys.append(y_f[pl.ds(pl.multiple_of(k * SUB, SUB), SUB), :] + terms[0])
            start = pl.multiple_of(p * piece + index * 2 * SUB, 2 * SUB)
            both = jnp.concatenate(ys, axis=0).astype(jnp.bfloat16)
            gath[me_c, pl.ds(start, 2 * SUB), :] = both
            return tuple(carry)

        carry = lax.fori_loop(0, piece // SUB // 2, pair, carry)
        go_up(me_c, 1, p).start()
        go_dn(me_c, 1, p).start()
        across(me_c, 0, 0, p).start()
        return carry

    lax.fori_loop(0, PIECES, finish, entering)

    for n in range(orders):
        parts[me_s, n : n + 1, :] = jnp.sum(
            l_bc[n] + b_bc[n] * c_bc[n], axis=0, keepdims=True
        )
    for hop in range(1, nseq):
        to_peer(parts, pt_send, pt_recv, hop).start()

    def multiply(chip, h):
        where = pl.ds(h * (rows // 2), rows // 2)
        block = jnp.concatenate([gath[chip * 2, where, :], gath[chip * 2 + 1, where, :]], axis=1)
        columns = pl.ds(pl.multiple_of(chip * 2 * lanes, 2 * lanes), 2 * lanes)
        acc[where, :] += lax.dot_general(
            block, w_v[:, columns], (((1,), (1,)), ((), ())), preferred_element_type=jnp.float32
        )

    def wait_partner(chip, d, s, h):
        slot = chip * 2 + (1 - core)
        for p in range(h * PIECES // 2, (h + 1) * PIECES // 2):
            across(slot, d, s, p).wait_recv()

    loads[5].wait()

    def ring_step(s, _):
        up = chip_up(s) * 2 + core
        dn = chip_dn(s) * 2 + core
        for p in range(PIECES):
            go_up(up, s, p).wait_recv()
            if p < PIECES // 2:
                go_up(up, s + 1, p).start()
            else:
                @pl.when(s < half - 1)
                def _():
                    go_up(up, s + 1, p).start()
            across(up, 0, s, p).start()
            go_dn(dn, s, p).wait_recv()
            if p >= PIECES // 2:
                go_dn(dn, s + 1, p).start()
            else:
                @pl.when(s < half - 1)
                def _():
                    go_dn(dn, s + 1, p).start()
            across(dn, 1, s, p).start()
            if p < 2:
                wait_partner(chip_up(s - 1), 0, s - 1, p)
                multiply(chip_up(s - 1), p)
            elif p < 4:
                @pl.when(s >= 2)
                def _():
                    wait_partner(chip_dn(s - 1), 1, s - 1, p - 2)
                    multiply(chip_dn(s - 1), p - 2)
        return 0

    lax.fori_loop(1, half, ring_step, 0)

    far = chip_up(half)
    near_up, near_dn = chip_up(half - 1), chip_dn(half - 1)
    for i in range(PIECES // 2):
        go_up(far * 2 + core, half, i).wait_recv()
        across(far * 2 + core, 0, half, i).start()
        go_dn(far * 2 + core, half, i + PIECES // 2).wait_recv()
        across(far * 2 + core, 0, half, i + PIECES // 2).start()
        wait_partner(near_up, 0, half - 1, i)
        multiply(near_up, i)
    for i in range(2):
        wait_partner(near_dn, 1, half - 1, i)
        multiply(near_dn, i)

    for hop in range(1, nseq):
        from_peer(parts, pt_send, pt_recv, hop).wait_recv()
    total = parts[0]
    for other in range(1, nseq):
        total = total + parts[other]
    total = total * jnp.sqrt(2.0 * dec_t[...]) * scale_len
    rg_ref[...] = jnp.transpose(total)

    for i in range(2):
        wait_partner(far, 0, half, i)
        multiply(far, i)

    for k in range(steps):
        nat[pl.ds(steps - 1 - k, SUB, stride=steps), :] = acc[k * SUB : (k + 1) * SUB, :]
    out_ref[...] = nat[...].astype(out_ref.dtype)

    for hop in range(1, nseq):
        to_peer(states, st_send, st_recv, hop).wait_send()
        to_peer(parts, pt_send, pt_recv, hop).wait_send()
    for p in range(PIECES):
        across(me_c, 0, 0, p).wait_send()

    def drain(s, _):
        for p in range(PIECES):
            go_up(me_c, s, p).wait_send()
            go_dn(me_c, s, p).wait_send()
            across(me_c, 0, s, p).wait_send()
            across(me_c, 1, s, p).wait_send()
        return 0

    lax.fori_loop(1, half, drain, 0)
    for p in range(PIECES):
        across(me_c, 0, half, p).wait_send()
        if p < PIECES // 2:
            go_up(me_c, half, p).wait_send()
        else:
            go_dn(me_c, half, p).wait_send()


def per_device(nseq, nz, grad_out, activation, residues, decay, skip, in_weight):
    rows, lanes = grad_out.shape
    orders = decay.shape[1]
    features, width = in_weight.shape
    f32, bf16 = jnp.float32, jnp.bfloat16
    half = nz // 2
    dma = pltpu.SemaphoreType.DMA
    any_spec = pl.BlockSpec(memory_space=pl.ANY)
    vmem_spec = pl.BlockSpec(memory_space=pltpu.VMEM)
    spread = pltpu.VMEM((orders, SUB, lanes), f32)
    return pl.pallas_call(
        functools.partial(kernel, nseq, nz, 1.0 / math.sqrt(nseq * rows)),
        out_shape=(
            jax.ShapeDtypeStruct((rows, features), bf16),
            jax.ShapeDtypeStruct((lanes, orders), f32),
        ),
        in_specs=[any_spec] * 6,
        out_specs=(vmem_spec, vmem_spec),
        scratch_shapes=[
            pltpu.VMEM((nz * 2, rows, lanes), bf16),
            pltpu.VMEM((features, width), bf16),
            pltpu.VMEM((rows, lanes), bf16),
            pltpu.VMEM((rows, lanes), bf16),
            pltpu.VMEM((lanes, orders), f32),
            pltpu.VMEM((lanes, orders), f32),
            pltpu.VMEM((1, lanes), f32),
            pltpu.VMEM((rows, lanes), f32),
            pltpu.VMEM((rows, lanes), f32),
            pltpu.VMEM((rows, lanes), f32),
            pltpu.VMEM((rows, features), f32),
            pltpu.VMEM((rows, features), f32),
            spread,
            spread,
            spread,
            spread,
            spread,
            spread,
            pltpu.VMEM((orders, lanes), f32),
            pltpu.VMEM((nseq, orders, lanes), f32),
            pltpu.VMEM((nseq, orders, lanes), f32),
            dma((6,)),
            dma((nseq,)),
            dma((nseq,)),
            dma((nseq,)),
            dma((nseq,)),
            dma((half + 1, PIECES)),
            dma((half + 1, PIECES)),
            dma((half + 1, PIECES)),
            dma((half + 1, PIECES)),
            dma((2, half + 1, PIECES)),
            dma((2, half + 1, PIECES)),
        ],
        compiler_params=pltpu.CompilerParams(
            collective_id=0, has_side_effects=True, vmem_limit_bytes=40 * 2**20
        ),
        name="modal_backward",
    )(grad_out, activation, residues, decay, skip.reshape(1, lanes), in_weight)


def solution(mesh):
    nseq = mesh.shape["seq"]
    nz = mesh.shape["chan"] // 2
    return jax.shard_map(
        functools.partial(per_device, nseq, nz),
        mesh=mesh,
        in_specs=(
            P("seq", "chan"),
            P("seq", "chan"),
            P("chan", None),
            P("chan", None),
            P("chan"),
            P("chan", None),
        ),
        out_specs=(P("seq", "chan"), P("chan", None)),
        check_vma=False,
    )
```

```python
import functools
import math

import jax
import jax.numpy as jnp
from jax import lax
from jax.experimental import pallas as pl
from jax.experimental.pallas import tpu as pltpu
from jax.sharding import PartitionSpec as P

MESH = pl.DeviceIdType.MESH
SUB = 8
PIECES = 4


def kernel(
    nseq,
    nz,
    scale_len,
    g_hbm,
    act_hbm,
    res_hbm,
    dec_hbm,
    skip_hbm,
    w_hbm,
    out_ref,
    rg_ref,
    gath,
    w_v,
    g_b,
    act_b,
    res_v,
    dec_v,
    skip_v,
    g_f,
    act_f,
    y_f,
    acc,
    send_acc,
    inbox,
    nat,
    a_bc,
    r_bc,
    z_bc,
    l_bc,
    b_bc,
    c_bc,
    states,
    parts,
    load_sem,
    w_sem,
    w_send,
    w_recv,
    st_send,
    st_recv,
    pt_send,
    pt_recv,
    ring_send,
    ring_recv,
    pr_send,
    pr_recv,
    in_send,
    in_recv,
):
    rows, lanes = g_b.shape
    orders = dec_v.shape[0]
    features = w_hbm.shape[0]
    steps = rows // SUB
    half = nz // 2
    piece = rows // PIECES
    me_s = lax.axis_index("seq")
    me_c = lax.axis_index("chan")
    me_z = me_c // 2
    core = me_c % 2
    partner = me_z * 2 + (1 - core)
    onward = ((me_z + nz + 1 - 2 * core) % nz) * 2 + core
    source = ((me_z + nz - 1 + 2 * core) % nz) * 2 + core

    def chip_at(s, side=core):
        return (me_z + nz + (2 * side - 1) * s) % nz

    def load(src, dst, index):
        return pltpu.make_async_copy(src, dst, load_sem.at[index])

    loads = [
        load(g_hbm, g_b, 0),
        load(dec_hbm, dec_v, 1),
        load(res_hbm, res_v, 2),
        load(skip_hbm, skip_v, 3),
        load(act_hbm, act_b, 4),
    ]
    barrier = pltpu.get_barrier_semaphore()
    for hop in range(1, nseq):
        pl.semaphore_signal(
            barrier, inc=1, device_id=((me_s + hop) % nseq, me_c), device_id_type=MESH
        )
    for other in (partner, source):
        pl.semaphore_signal(barrier, inc=1, device_id=(me_s, other), device_id_type=MESH)
    for copy in loads:
        copy.start()

    def chip_columns(chip):
        return pl.ds(pl.multiple_of(chip * 2 * lanes, 2 * lanes), 2 * lanes)

    def own_weight(s):
        return pltpu.make_async_copy(
            w_hbm.at[:, chip_columns(chip_at(s))], w_v.at[s, pl.ds(0, features), :], w_sem.at[s]
        )

    def partner_weight(s):
        return pltpu.make_async_remote_copy(
            src_ref=w_hbm.at[:, chip_columns(chip_at(s, 1 - core))],
            dst_ref=w_v.at[s, pl.ds(features, features), :],
            send_sem=w_send.at[s],
            recv_sem=w_recv.at[s],
            device_id=(me_s, partner),
            device_id_type=MESH,
        )

    for s in range(half + 1):
        own_weight(s).start()

    loads[1].wait()
    loads[2].wait()
    loads[3].wait()
    decay = dec_v[...]
    strength = res_v[...] * jnp.sqrt(2.0 * decay)
    pole = jnp.exp(-decay)
    for n in range(orders):
        a_bc[n] = jnp.broadcast_to(pole[n : n + 1], (SUB, lanes))
        r_bc[n] = jnp.broadcast_to(strength[n : n + 1], (SUB, lanes))
    acc[...] = jnp.zeros_like(acc)
    send_acc[...] = jnp.zeros_like(send_acc)

    loads[0].wait()
    loads[4].wait()
    g_f[...] = g_b[...].astype(jnp.float32)
    act_f[...] = act_b[...].astype(jnp.float32)

    zero = jnp.zeros((SUB, lanes), jnp.float32)
    skip_row = jnp.broadcast_to(skip_v[...], (SUB, lanes))
    group = orders // 2
    unroll = 2
    for part in range(2):
        chosen = range(part * group, (part + 1) * group)
        poles = [a_bc[n] for n in chosen]
        gains = [r_bc[n] for n in chosen]

        def scan(index, carry, poles=poles, gains=gains, part=part):
            state, total = list(carry[0]), list(carry[1])
            for inner in range(unroll):
                k = index * unroll + inner
                g_row = g_f[pl.ds(steps - 1 - k, SUB, stride=steps), :]
                act_row = act_f[pl.ds(steps - 1 - k, SUB, stride=steps), :]
                where = pl.ds(pl.multiple_of(k * SUB, SUB), SUB)
                y = skip_row * g_row if part == 0 else y_f[where, :]
                terms = []
                for m in range(group):
                    state[m] = g_row + poles[m] * state[m]
                    terms.append(gains[m] * state[m])
                    total[m] = total[m] + act_row * state[m]
                while len(terms) > 1:
                    terms = [terms[i] + terms[i + 1] for i in range(0, len(terms), 2)]
                y_f[where, :] = y + terms[0]
            return tuple(state), tuple(total)

        state, total = lax.fori_loop(
            0, steps // unroll, scan, ((zero,) * group, (zero,) * group)
        )
        for m, n in enumerate(chosen):
            z_bc[n] = state[m]
            l_bc[n] = total[m]

    row = lax.broadcasted_iota(jnp.int32, (SUB, lanes), 0)
    for n in range(orders):
        rate = jnp.broadcast_to(dec_v[n : n + 1, :], (SUB, lanes))
        state = z_bc[n]
        shift = 1
        while shift < SUB:
            moved = jnp.where(row < SUB - shift, pltpu.roll(state, SUB - shift, 0), 0.0)
            state = state + jnp.exp(rate * float(-steps * shift)) * moved
            shift *= 2
        states[me_s, n : n + 1, :] = state[0:1]
        z_bc[n] = jnp.where(row < SUB - 1, pltpu.roll(state, SUB - 1, 0), 0.0)

    pl.semaphore_wait(barrier, nseq - 1 + 2)

    def to_peer(buffer, send, recv, hop):
        peer = (me_s + hop) % nseq
        return pltpu.make_async_remote_copy(
            src_ref=buffer.at[me_s],
            dst_ref=buffer.at[me_s],
            send_sem=send.at[hop],
            recv_sem=recv.at[me_s],
            device_id=(peer, me_c),
            device_id_type=MESH,
        )

    def from_peer(buffer, send, recv, hop):
        peer = (me_s + hop) % nseq
        return pltpu.make_async_remote_copy(
            src_ref=buffer.at[peer],
            dst_ref=buffer.at[peer],
            send_sem=send.at[hop],
            recv_sem=recv.at[peer],
            device_id=(peer, me_c),
            device_id_type=MESH,
        )

    for hop in range(1, nseq):
        to_peer(states, st_send, st_recv, hop).start()
    for s in range(half + 1):
        partner_weight(s).start()

    def weigh(index, carry):
        carry = list(carry)
        for inner in range(unroll):
            j = index * unroll + inner
            act_row = act_f[pl.ds(j, SUB, stride=steps), :]
            for n in range(orders):
                carry[n] = a_bc[n] * (carry[n] + act_row)
        return tuple(carry)

    weights = lax.fori_loop(0, steps // unroll, weigh, (zero,) * orders)
    distance = (SUB - 1 - row).astype(jnp.float32) * float(steps)
    for n in range(orders):
        b_bc[n] = weights[n]
        rate = jnp.broadcast_to(dec_v[n : n + 1, :], (SUB, lanes))
        c_bc[n] = jnp.exp(-rate * distance)
    block_pole = jnp.exp(dec_v[...] * float(-rows))

    for hop in range(1, nseq):
        from_peer(states, st_send, st_recv, hop).wait_recv()
    enter = jnp.zeros((orders, lanes), jnp.float32)
    for later in range(nseq - 1, 0, -1):
        enter = jnp.where(later > me_s, states[later] + block_pole * enter, enter)
    for n in range(orders):
        c_bc[n] = z_bc[n] + c_bc[n] * jnp.broadcast_to(enter[n : n + 1], (SUB, lanes))

    def rows_of(p):
        return pl.ds(pl.multiple_of(p * piece, piece), piece)

    def pass_on(chip, side, s, p):
        view = gath.at[chip * 2 + side, rows_of(p), :]
        return pltpu.make_async_remote_copy(
            src_ref=view,
            dst_ref=view,
            send_sem=ring_send.at[s, side, p],
            recv_sem=ring_recv.at[s, side, p],
            device_id=(me_s, onward),
            device_id_type=MESH,
        )

    def across(side, p):
        view = gath.at[me_z * 2 + side, rows_of(p), :]
        return pltpu.make_async_remote_copy(
            src_ref=view,
            dst_ref=view,
            send_sem=pr_send.at[p],
            recv_sem=pr_recv.at[p],
            device_id=(me_s, partner),
            device_id_type=MESH,
        )

    def hand_over(p):
        return pltpu.make_async_remote_copy(
            src_ref=send_acc.at[rows_of(p), :],
            dst_ref=inbox.at[rows_of(p), :],
            send_sem=in_send.at[p],
            recv_sem=in_recv.at[p],
            device_id=(me_s, partner),
            device_id_type=MESH,
        )

    poles = [a_bc[n] for n in range(orders)]
    entering = tuple(r_bc[n] * c_bc[n] for n in range(orders))

    def finish(p, carry):
        def pair(index, carry):
            ys = []
            for inner in range(2):
                k = p * (piece // SUB) + index * 2 + inner
                carry = [poles[n] * carry[n] for n in range(orders)]
                terms = list(carry)
                while len(terms) > 1:
                    terms = [terms[i] + terms[i + 1] for i in range(0, len(terms), 2)]
                ys.append(y_f[pl.ds(pl.multiple_of(k * SUB, SUB), SUB), :] + terms[0])
            start = pl.multiple_of(p * piece + index * 2 * SUB, 2 * SUB)
            both = jnp.concatenate(ys, axis=0).astype(jnp.bfloat16)
            gath[me_c, pl.ds(start, 2 * SUB), :] = both
            return tuple(carry)

        carry = lax.fori_loop(0, piece // SUB // 2, pair, carry)
        pass_on(me_z, core, 1, p).start()
        across(core, p).start()
        return carry

    lax.fori_loop(0, PIECES, finish, entering)

    for n in range(orders):
        parts[me_s, n : n + 1, :] = jnp.sum(
            l_bc[n] + b_bc[n] * c_bc[n], axis=0, keepdims=True
        )
    for hop in range(1, nseq):
        to_peer(parts, pt_send, pt_recv, hop).start()

    for p in range(PIECES):
        across(1 - core, p).wait_recv()
        pass_on(me_z, 1 - core, 1, p).start()
    for s in range(half + 1):
        own_weight(s).wait()
        partner_weight(s).wait_recv()

    def multiply(s, p):
        chip = chip_at(s)
        where = rows_of(p)
        block = jnp.concatenate([gath[chip * 2, where, :], gath[chip * 2 + 1, where, :]], axis=1)
        both = lax.dot_general(
            block, w_v[s], (((1,), (1,)), ((), ())), preferred_element_type=jnp.float32
        )
        acc[where, :] += both[:, :features]
        send_acc[where, :] += both[:, features:]

    def ring_step(s, _):
        chip = chip_at(s)
        for turn in range(2):
            side = core if turn == 0 else 1 - core
            for p in range(PIECES):
                pass_on(chip, side, s, p).wait_recv()

                @pl.when((s < half - 1) | (p // (PIECES // 2) == core))
                def _(side=side, p=p):
                    pass_on(chip, side, s + 1, p).start()

                index = turn * PIECES + p
                if index % 2 == 1:
                    u = index // 2

                    @pl.when((s >= 2) | (u // (PIECES // 2) == core))
                    def _(u=u):
                        multiply(s - 1, u)

        return 0

    lax.fori_loop(1, half, ring_step, 0)

    ours = [core * (PIECES // 2) + i for i in range(PIECES // 2)]
    theirs = [(1 - core) * (PIECES // 2) + i for i in range(PIECES // 2)]
    for p in theirs:
        multiply(half - 1, p)
    for p in theirs:
        hand_over(p).start()
    for p in ours:
        multiply(half - 1, p)

    for hop in range(1, nseq):
        from_peer(parts, pt_send, pt_recv, hop).wait_recv()
    total = parts[0]
    for other in range(1, nseq):
        total = total + parts[other]
    rg_ref[...] = total * jnp.sqrt(2.0 * dec_v[...]) * scale_len

    far = chip_at(half)
    for p in ours:
        pass_on(far, core, half, p).wait_recv()
    for p in ours:
        pass_on(far, 1 - core, half, p).wait_recv()
        multiply(half, p)
        hand_over(p).start()

    def deliver(p):
        hand_over(p).wait_recv()
        span = piece // SUB
        for i in range(span):
            k = p * span + i
            where = pl.ds(pl.multiple_of(k * SUB, SUB), SUB)
            nat[pl.ds(steps - 1 - k, SUB, stride=steps), :] = acc[where, :] + inbox[where, :]
        for b in range(SUB):
            where = pl.ds(pl.multiple_of(b * steps + steps - (p + 1) * span, span), span)
            out_ref[where, :] = nat[where, :].astype(out_ref.dtype)

    for p in ours + theirs:
        deliver(p)

    for hop in range(1, nseq):
        to_peer(states, st_send, st_recv, hop).wait_send()
        to_peer(parts, pt_send, pt_recv, hop).wait_send()
    for s in range(half + 1):
        partner_weight(s).wait_send()
    for p in range(PIECES):
        across(core, p).wait_send()
        hand_over(p).wait_send()

    def drain(s, _):
        for side in range(2):
            for p in range(PIECES):
                pass_on(me_z, side, s, p).wait_send()
        return 0

    lax.fori_loop(1, half, drain, 0)
    for side in range(2):
        for p in ours:
            pass_on(me_z, side, half, p).wait_send()


def per_device(nseq, nz, grad_out, activation, residues, decay, skip, in_weight):
    rows, lanes = grad_out.shape
    orders = decay.shape[1]
    features, width = in_weight.shape
    f32, bf16 = jnp.float32, jnp.bfloat16
    half = nz // 2
    dma = pltpu.SemaphoreType.DMA
    hbm_spec = pl.BlockSpec(memory_space=pltpu.HBM)
    vmem_spec = pl.BlockSpec(memory_space=pltpu.VMEM)
    spread = pltpu.VMEM((orders, SUB, lanes), f32)
    total = pltpu.VMEM((rows, features), f32)
    arrays = (grad_out, activation, residues.T, decay.T, skip.reshape(1, lanes), in_weight)
    input_grad, residue_grad = pl.pallas_call(
        functools.partial(kernel, nseq, nz, 1.0 / math.sqrt(nseq * rows)),
        out_shape=(
            jax.ShapeDtypeStruct((rows, features), bf16),
            jax.ShapeDtypeStruct((orders, lanes), f32),
        ),
        in_specs=[hbm_spec] * 6,
        out_specs=(vmem_spec, vmem_spec),
        scratch_shapes=[
            pltpu.VMEM((nz * 2, rows, lanes), bf16),
            pltpu.VMEM((half + 1, 2 * features, 2 * lanes), bf16),
            pltpu.VMEM((rows, lanes), bf16),
            pltpu.VMEM((rows, lanes), bf16),
            pltpu.VMEM((orders, lanes), f32),
            pltpu.VMEM((orders, lanes), f32),
            pltpu.VMEM((1, lanes), f32),
            pltpu.VMEM((rows, lanes), f32),
            pltpu.VMEM((rows, lanes), f32),
            pltpu.VMEM((rows, lanes), f32),
            total,
            total,
            total,
            total,
            spread,
            spread,
            spread,
            spread,
            spread,
            spread,
            pltpu.VMEM((nseq, orders, lanes), f32),
            pltpu.VMEM((nseq, orders, lanes), f32),
            dma((5,)),
            dma((half + 1,)),
            dma((half + 1,)),
            dma((half + 1,)),
            dma((nseq,)),
            dma((nseq,)),
            dma((nseq,)),
            dma((nseq,)),
            dma((half + 1, 2, PIECES)),
            dma((half + 1, 2, PIECES)),
            dma((PIECES,)),
            dma((PIECES,)),
            dma((PIECES,)),
            dma((PIECES,)),
        ],
        compiler_params=pltpu.CompilerParams(
            collective_id=0, has_side_effects=True, vmem_limit_bytes=40 * 2**20
        ),
        name="modal_backward",
    )(*(pltpu.with_memory_space_constraint(x, pltpu.HBM) for x in arrays))
    return (input_grad, residue_grad.T)


def solution(mesh):
    nseq = mesh.shape["seq"]
    nz = mesh.shape["chan"] // 2
    return jax.shard_map(
        functools.partial(per_device, nseq, nz),
        mesh=mesh,
        in_specs=(
            P("seq", "chan"),
            P("seq", "chan"),
            P("chan", None),
            P("chan", None),
            P("chan"),
            P("chan", None),
        ),
        out_specs=(P("seq", "chan"), P("chan", None)),
        check_vma=False,
    )
```

```python
import functools
import math

import jax
import jax.numpy as jnp
from jax import lax
from jax.experimental import pallas as pl
from jax.experimental.pallas import tpu as pltpu
from jax.sharding import PartitionSpec as P

MESH = pl.DeviceIdType.MESH
SUB = 8
PIECES = 4


def far_first(nseq):
    edge = max(math.isqrt(nseq), 1)

    def away(hop):
        across, along = divmod(hop, edge)
        return min(across, edge - across) + min(along, edge - along)

    return sorted(range(1, nseq), key=lambda hop: -away(hop))


def kernel(
    nseq,
    nz,
    scale_len,
    g_hbm,
    act_hbm,
    res_hbm,
    dec_hbm,
    skip_hbm,
    w_hbm,
    out_ref,
    rg_ref,
    gath,
    w_v,
    g_b,
    act_b,
    res_v,
    dec_v,
    skip_v,
    g_f,
    act_f,
    y_f,
    acc,
    send_acc,
    inbox,
    nat,
    a_bc,
    r_bc,
    z_bc,
    l_bc,
    b_bc,
    c_bc,
    e_bc,
    states,
    parts,
    load_sem,
    w_sem,
    w_send,
    w_recv,
    st_send,
    st_recv,
    pt_send,
    pt_recv,
    ring_send,
    ring_recv,
    pr_send,
    pr_recv,
    in_send,
    in_recv,
):
    rows, lanes = g_b.shape
    orders = dec_v.shape[0]
    features = w_hbm.shape[0]
    steps = rows // SUB
    half = nz // 2
    piece = rows // PIECES
    me_s = lax.axis_index("seq")
    me_c = lax.axis_index("chan")
    me_z = me_c // 2
    core = me_c % 2
    partner = me_z * 2 + (1 - core)
    onward = ((me_z + nz + 1 - 2 * core) % nz) * 2 + core
    source = ((me_z + nz - 1 + 2 * core) % nz) * 2 + core

    def chip_at(s, side=core):
        return (me_z + nz + (2 * side - 1) * s) % nz

    def load(src, dst, index):
        return pltpu.make_async_copy(src, dst, load_sem.at[index])

    loads = [
        load(g_hbm, g_b, 0),
        load(dec_hbm, dec_v, 1),
        load(res_hbm, res_v, 2),
        load(skip_hbm, skip_v, 3),
        load(act_hbm, act_b, 4),
    ]
    barrier = pltpu.get_barrier_semaphore()
    loads[0].start()
    loads[1].start()
    loads[2].start()
    states[...] = jnp.zeros_like(states)
    hops = far_first(nseq)
    for hop in hops:

        @pl.when((me_s + hop) % nseq > me_s)
        def _(hop=hop):
            pl.semaphore_signal(
                barrier, inc=1, device_id=((me_s + hop) % nseq, me_c), device_id_type=MESH
            )

    for other in (source, partner):
        pl.semaphore_signal(barrier, inc=1, device_id=(me_s, other), device_id_type=MESH)
    loads[3].start()
    loads[4].start()

    def chip_columns(chip):
        return pl.ds(pl.multiple_of(chip * 2 * lanes, 2 * lanes), 2 * lanes)

    def own_weight(s):
        return pltpu.make_async_copy(
            w_hbm.at[:, chip_columns(chip_at(s))], w_v.at[s, pl.ds(0, features), :], w_sem.at[s]
        )

    def partner_weight(s):
        return pltpu.make_async_remote_copy(
            src_ref=w_hbm.at[:, chip_columns(chip_at(s, 1 - core))],
            dst_ref=w_v.at[s, pl.ds(features, features), :],
            send_sem=w_send.at[s],
            recv_sem=w_recv.at[s],
            device_id=(me_s, partner),
            device_id_type=MESH,
        )

    for s in range(half + 1):
        own_weight(s).start()
    acc[...] = jnp.zeros_like(acc)
    send_acc[...] = jnp.zeros_like(send_acc)

    loads[1].wait()
    decay = dec_v[...]
    pole = jnp.exp(-decay)
    for n in range(orders):
        a_bc[n] = jnp.broadcast_to(pole[n : n + 1], (SUB, lanes))

    zero = jnp.zeros((SUB, lanes), jnp.float32)
    loads[0].wait()
    g_f[...] = g_b[...].astype(jnp.float32)
    unroll = 2

    def gather_states(index, state):
        for inner in range(unroll):
            k = index * unroll + inner
            g_row = g_f[pl.ds(steps - 1 - k, SUB, stride=steps), :]
            state = [g_row + a_bc[n] * state[n] for n in range(orders)]
        return tuple(state)

    ends = lax.fori_loop(0, steps // unroll, gather_states, (zero,) * orders)

    row = lax.broadcasted_iota(jnp.int32, (SUB, lanes), 0)
    for n in range(orders):
        rate = jnp.broadcast_to(dec_v[n : n + 1, :], (SUB, lanes))
        state = ends[n]
        shift = 1
        while shift < SUB:
            moved = jnp.where(row < SUB - shift, pltpu.roll(state, SUB - shift, 0), 0.0)
            state = state + jnp.exp(rate * float(-steps * shift)) * moved
            shift *= 2
        states[me_s, n : n + 1, :] = state[0:1]
        z_bc[n] = jnp.where(row < SUB - 1, pltpu.roll(state, SUB - 1, 0), 0.0)

    pl.semaphore_wait(barrier, me_s + 2)

    def to_peer(buffer, send, recv, hop):
        peer = (me_s + hop) % nseq
        return pltpu.make_async_remote_copy(
            src_ref=buffer.at[me_s],
            dst_ref=buffer.at[me_s],
            send_sem=send.at[hop],
            recv_sem=recv.at[me_s],
            device_id=(peer, me_c),
            device_id_type=MESH,
        )

    def from_peer(buffer, send, recv, hop):
        peer = (me_s + hop) % nseq
        return pltpu.make_async_remote_copy(
            src_ref=buffer.at[peer],
            dst_ref=buffer.at[peer],
            send_sem=send.at[hop],
            recv_sem=recv.at[peer],
            device_id=(peer, me_c),
            device_id_type=MESH,
        )

    for hop in hops:

        @pl.when((me_s + hop) % nseq < me_s)
        def _(hop=hop):
            to_peer(states, st_send, st_recv, hop).start()

    for s in range(half + 1):
        partner_weight(s).start()

    loads[2].wait()
    loads[3].wait()
    loads[4].wait()
    strength = res_v[...] * jnp.sqrt(2.0 * dec_v[...])
    for n in range(orders):
        r_bc[n] = jnp.broadcast_to(strength[n : n + 1], (SUB, lanes))
    act_f[...] = act_b[...].astype(jnp.float32)
    skip_row = jnp.broadcast_to(skip_v[...], (SUB, lanes))
    group = orders // 2
    for part in range(2):
        chosen = range(part * group, (part + 1) * group)
        poles = [a_bc[n] for n in chosen]
        gains = [r_bc[n] for n in chosen]

        def scan(index, carry, poles=poles, gains=gains, part=part):
            state, total = list(carry[0]), list(carry[1])
            for inner in range(unroll):
                k = index * unroll + inner
                g_row = g_f[pl.ds(steps - 1 - k, SUB, stride=steps), :]
                act_row = act_f[pl.ds(steps - 1 - k, SUB, stride=steps), :]
                where = pl.ds(pl.multiple_of(k * SUB, SUB), SUB)
                y = skip_row * g_row if part == 0 else y_f[where, :]
                terms = []
                for m in range(group):
                    state[m] = g_row + poles[m] * state[m]
                    terms.append(gains[m] * state[m])
                    total[m] = total[m] + act_row * state[m]
                while len(terms) > 1:
                    terms = [terms[i] + terms[i + 1] for i in range(0, len(terms), 2)]
                y_f[where, :] = y + terms[0]
            return tuple(state), tuple(total)

        _, total = lax.fori_loop(
            0, steps // unroll, scan, ((zero,) * group, (zero,) * group)
        )
        for m, n in enumerate(chosen):
            l_bc[n] = total[m]

    def weigh(index, carry):
        carry = list(carry)
        for inner in range(unroll):
            j = index * unroll + inner
            act_row = act_f[pl.ds(j, SUB, stride=steps), :]
            for n in range(orders):
                carry[n] = a_bc[n] * (carry[n] + act_row)
        return tuple(carry)

    weights = lax.fori_loop(0, steps // unroll, weigh, (zero,) * orders)
    distance = (SUB - 1 - row).astype(jnp.float32) * float(steps)
    for n in range(orders):
        b_bc[n] = weights[n]
        rate = jnp.broadcast_to(dec_v[n : n + 1, :], (SUB, lanes))
        c_bc[n] = jnp.exp(-rate * distance)
    for later in range(1, nseq):
        blocks = jnp.maximum(later - me_s - 1, 0).astype(jnp.float32) * float(rows)
        e_bc[later] = jnp.where(later > me_s, jnp.exp(dec_v[...] * -blocks), 0.0)

    for hop in hops:

        @pl.when((me_s + hop) % nseq > me_s)
        def _(hop=hop):
            from_peer(states, st_send, st_recv, hop).wait_recv()

    terms = [e_bc[later] * states[later] for later in range(1, nseq)]
    while len(terms) > 1:
        terms = [sum(terms[i : i + 2]) for i in range(0, len(terms), 2)]
    enter = terms[0]
    for n in range(orders):
        c_bc[n] = z_bc[n] + c_bc[n] * jnp.broadcast_to(enter[n : n + 1], (SUB, lanes))

    def rows_of(p):
        return pl.ds(pl.multiple_of(p * piece, piece), piece)

    def pass_on(chip, side, s, p):
        view = gath.at[chip * 2 + side, rows_of(p), :]
        return pltpu.make_async_remote_copy(
            src_ref=view,
            dst_ref=view,
            send_sem=ring_send.at[s, side, p],
            recv_sem=ring_recv.at[s, side, p],
            device_id=(me_s, onward),
            device_id_type=MESH,
        )

    def across(side, p):
        view = gath.at[me_z * 2 + side, rows_of(p), :]
        return pltpu.make_async_remote_copy(
            src_ref=view,
            dst_ref=view,
            send_sem=pr_send.at[p],
            recv_sem=pr_recv.at[p],
            device_id=(me_s, partner),
            device_id_type=MESH,
        )

    def hand_over(p):
        return pltpu.make_async_remote_copy(
            src_ref=send_acc.at[rows_of(p), :],
            dst_ref=inbox.at[rows_of(p), :],
            send_sem=in_send.at[p],
            recv_sem=in_recv.at[p],
            device_id=(me_s, partner),
            device_id_type=MESH,
        )

    poles = [a_bc[n] for n in range(orders)]
    entering = tuple(r_bc[n] * c_bc[n] for n in range(orders))

    def finish(p, carry):
        def pair(index, carry):
            ys = []
            for inner in range(2):
                k = p * (piece // SUB) + index * 2 + inner
                carry = [poles[n] * carry[n] for n in range(orders)]
                terms = list(carry)
                while len(terms) > 1:
                    terms = [terms[i] + terms[i + 1] for i in range(0, len(terms), 2)]
                ys.append(y_f[pl.ds(pl.multiple_of(k * SUB, SUB), SUB), :] + terms[0])
            start = pl.multiple_of(p * piece + index * 2 * SUB, 2 * SUB)
            both = jnp.concatenate(ys, axis=0).astype(jnp.bfloat16)
            gath[me_c, pl.ds(start, 2 * SUB), :] = both
            return tuple(carry)

        carry = lax.fori_loop(0, piece // SUB // 2, pair, carry)
        pass_on(me_z, core, 1, p).start()
        across(core, p).start()
        return carry

    lax.fori_loop(0, PIECES, finish, entering)

    for n in range(orders):
        parts[me_s, n : n + 1, :] = jnp.sum(
            l_bc[n] + b_bc[n] * c_bc[n], axis=0, keepdims=True
        )
    for hop in range(1, nseq):
        to_peer(parts, pt_send, pt_recv, hop).start()

    for p in range(PIECES):
        across(1 - core, p).wait_recv()
        pass_on(me_z, 1 - core, 1, p).start()
    for s in range(half + 1):
        own_weight(s).wait()
        partner_weight(s).wait_recv()

    def multiply(s, p):
        chip = chip_at(s)
        where = rows_of(p)
        block = jnp.concatenate([gath[chip * 2, where, :], gath[chip * 2 + 1, where, :]], axis=1)
        both = lax.dot_general(
            block, w_v[s], (((1,), (1,)), ((), ())), preferred_element_type=jnp.float32
        )
        acc[where, :] += both[:, :features]
        send_acc[where, :] += both[:, features:]

    def ring_step(s, _):
        chip = chip_at(s)
        for turn in range(2):
            side = core if turn == 0 else 1 - core
            for p in range(PIECES):
                pass_on(chip, side, s, p).wait_recv()

                @pl.when((s < half - 1) | (p // (PIECES // 2) == core))
                def _(side=side, p=p):
                    pass_on(chip, side, s + 1, p).start()

                index = turn * PIECES + p
                if index % 2 == 1:
                    u = index // 2

                    @pl.when((s >= 2) | (u // (PIECES // 2) == core))
                    def _(u=u):
                        multiply(s - 1, u)

        return 0

    lax.fori_loop(1, half, ring_step, 0)

    ours = [core * (PIECES // 2) + i for i in range(PIECES // 2)]
    theirs = [(1 - core) * (PIECES // 2) + i for i in range(PIECES // 2)]
    for p in theirs:
        multiply(half - 1, p)
    for p in theirs:
        hand_over(p).start()
    for p in ours:
        multiply(half - 1, p)

    for hop in range(1, nseq):
        from_peer(parts, pt_send, pt_recv, hop).wait_recv()
    total = parts[0]
    for other in range(1, nseq):
        total = total + parts[other]
    rg_ref[...] = total * jnp.sqrt(2.0 * dec_v[...]) * scale_len

    far = chip_at(half)
    for p in ours:
        pass_on(far, core, half, p).wait_recv()
    for p in ours:
        pass_on(far, 1 - core, half, p).wait_recv()
        multiply(half, p)
        hand_over(p).start()

    def deliver(p):
        hand_over(p).wait_recv()
        span = piece // SUB
        for i in range(span):
            k = p * span + i
            where = pl.ds(pl.multiple_of(k * SUB, SUB), SUB)
            nat[pl.ds(steps - 1 - k, SUB, stride=steps), :] = acc[where, :] + inbox[where, :]
        for b in range(SUB):
            where = pl.ds(pl.multiple_of(b * steps + steps - (p + 1) * span, span), span)
            out_ref[where, :] = nat[where, :].astype(out_ref.dtype)

    for p in ours + theirs:
        deliver(p)

    for hop in range(1, nseq):
        to_peer(parts, pt_send, pt_recv, hop).wait_send()

        @pl.when((me_s + hop) % nseq < me_s)
        def _(hop=hop):
            to_peer(states, st_send, st_recv, hop).wait_send()

    for s in range(half + 1):
        partner_weight(s).wait_send()
    for p in range(PIECES):
        across(core, p).wait_send()
        hand_over(p).wait_send()

    def drain(s, _):
        for side in range(2):
            for p in range(PIECES):
                pass_on(me_z, side, s, p).wait_send()
        return 0

    lax.fori_loop(1, half, drain, 0)
    for side in range(2):
        for p in ours:
            pass_on(me_z, side, half, p).wait_send()


def put_out(from_input_grad, from_residue_grad, input_grad, residue_grad, sem):
    copies = [
        pltpu.make_async_copy(from_input_grad, input_grad, sem.at[0]),
        pltpu.make_async_copy(from_residue_grad, residue_grad, sem.at[1]),
    ]
    for copy in copies:
        copy.start()
    for copy in copies:
        copy.wait()


def per_device(nseq, nz, grad_out, activation, residues, decay, skip, in_weight):
    rows, lanes = grad_out.shape
    orders = decay.shape[1]
    features, width = in_weight.shape
    f32, bf16 = jnp.float32, jnp.bfloat16
    half = nz // 2
    dma = pltpu.SemaphoreType.DMA
    hbm_spec = pl.BlockSpec(memory_space=pltpu.HBM)
    vmem_spec = pl.BlockSpec(memory_space=pltpu.VMEM)
    spread = pltpu.VMEM((orders, SUB, lanes), f32)
    total = pltpu.VMEM((rows, features), f32)
    arrays = (grad_out, activation, residues.T, decay.T, skip.reshape(1, lanes), in_weight)
    input_grad, residue_grad = pl.pallas_call(
        functools.partial(kernel, nseq, nz, 1.0 / math.sqrt(nseq * rows)),
        out_shape=(
            jax.ShapeDtypeStruct((rows, features), bf16),
            jax.ShapeDtypeStruct((orders, lanes), f32),
        ),
        in_specs=[hbm_spec] * 6,
        out_specs=(vmem_spec, vmem_spec),
        scratch_shapes=[
            pltpu.VMEM((nz * 2, rows, lanes), bf16),
            pltpu.VMEM((half + 1, 2 * features, 2 * lanes), bf16),
            pltpu.VMEM((rows, lanes), bf16),
            pltpu.VMEM((rows, lanes), bf16),
            pltpu.VMEM((orders, lanes), f32),
            pltpu.VMEM((orders, lanes), f32),
            pltpu.VMEM((1, lanes), f32),
            pltpu.VMEM((rows, lanes), f32),
            pltpu.VMEM((rows, lanes), f32),
            pltpu.VMEM((rows, lanes), f32),
            total,
            total,
            total,
            total,
            spread,
            spread,
            spread,
            spread,
            spread,
            spread,
            pltpu.VMEM((nseq, orders, lanes), f32),
            pltpu.VMEM((nseq, orders, lanes), f32),
            pltpu.VMEM((nseq, orders, lanes), f32),
            dma((5,)),
            dma((half + 1,)),
            dma((half + 1,)),
            dma((half + 1,)),
            dma((nseq,)),
            dma((nseq,)),
            dma((nseq,)),
            dma((nseq,)),
            dma((half + 1, 2, PIECES)),
            dma((half + 1, 2, PIECES)),
            dma((PIECES,)),
            dma((PIECES,)),
            dma((PIECES,)),
            dma((PIECES,)),
        ],
        compiler_params=pltpu.CompilerParams(
            collective_id=0, has_side_effects=True, vmem_limit_bytes=40 * 2**20
        ),
        name="modal_backward",
    )(*(pltpu.with_memory_space_constraint(x, pltpu.HBM) for x in arrays))
    input_grad, residue_grad = pl.pallas_call(
        put_out,
        out_shape=(
            jax.ShapeDtypeStruct((rows, features), bf16),
            jax.ShapeDtypeStruct((orders, lanes), f32),
        ),
        in_specs=[vmem_spec, vmem_spec],
        out_specs=(hbm_spec, hbm_spec),
        scratch_shapes=[dma((2,))],
        compiler_params=pltpu.CompilerParams(vmem_limit_bytes=2**20),
        name="put_out",
    )(input_grad, residue_grad)
    return (input_grad, residue_grad.T)


def solution(mesh):
    nseq = mesh.shape["seq"]
    nz = mesh.shape["chan"] // 2
    return jax.shard_map(
        functools.partial(per_device, nseq, nz),
        mesh=mesh,
        in_specs=(
            P("seq", "chan"),
            P("seq", "chan"),
            P("chan", None),
            P("chan", None),
            P("chan"),
            P("chan", None),
        ),
        out_specs=(P("seq", "chan"), P("chan", None)),
        check_vma=False,
    )
```

```python
import functools
import math

import jax
import jax.numpy as jnp
from jax import lax
from jax.experimental import pallas as pl
from jax.experimental.pallas import tpu as pltpu
from jax.sharding import PartitionSpec as P

MESH = pl.DeviceIdType.MESH
SUB = 8
TILT = 0
PIECES = 4


def reach_up(nz):
    return max((nz - 1) // 2 - TILT, 1)


def far_first(nseq):
    edge = max(math.isqrt(nseq), 1)

    def away(hop):
        across, along = divmod(hop, edge)
        return min(across, edge - across) + min(along, edge - along)

    return sorted(range(1, nseq), key=lambda hop: -away(hop))


def kernel(
    nseq,
    nz,
    scale_len,
    g_hbm,
    act_hbm,
    res_hbm,
    dec_hbm,
    skip_hbm,
    w_hbm,
    out_ref,
    rg_ref,
    gath,
    w_v,
    g_b,
    act_b,
    res_v,
    dec_v,
    skip_v,
    g_f,
    act_f,
    y_f,
    acc,
    send_acc,
    inbox,
    nat,
    a_bc,
    r_bc,
    z_bc,
    l_bc,
    b_bc,
    c_bc,
    e_bc,
    states,
    parts,
    load_sem,
    w_sem,
    w_send,
    w_recv,
    st_send,
    st_recv,
    pt_send,
    pt_recv,
    ring_send,
    ring_recv,
    pr_send,
    pr_recv,
    in_send,
    in_recv,
):
    rows, lanes = g_b.shape
    orders = dec_v.shape[0]
    features = w_hbm.shape[0]
    steps = rows // SUB
    ups = reach_up(nz)
    most = max(ups, nz - 1 - ups)
    piece = rows // PIECES
    me_s = lax.axis_index("seq")
    me_c = lax.axis_index("chan")
    me_z = me_c // 2
    core = me_c % 2
    partner = me_z * 2 + (1 - core)
    onward = ((me_z + nz + 1 - 2 * core) % nz) * 2 + core
    source = ((me_z + nz - 1 + 2 * core) % nz) * 2 + core

    last = ups + (nz - 1 - 2 * ups) * core

    def chip_at(s, side=core):
        return (me_z + nz + (2 * side - 1) * s) % nz

    def load(src, dst, index):
        return pltpu.make_async_copy(src, dst, load_sem.at[index])

    loads = [
        load(g_hbm, g_b, 0),
        load(dec_hbm, dec_v, 1),
        load(res_hbm, res_v, 2),
        load(skip_hbm, skip_v, 3),
        load(act_hbm, act_b, 4),
    ]
    barrier = pltpu.get_barrier_semaphore()
    loads[0].start()
    loads[1].start()
    loads[2].start()
    states[...] = jnp.zeros_like(states)
    hops = far_first(nseq)
    for hop in hops:

        @pl.when((me_s + hop) % nseq > me_s)
        def _(hop=hop):
            pl.semaphore_signal(
                barrier, inc=1, device_id=((me_s + hop) % nseq, me_c), device_id_type=MESH
            )

    for other in (source, partner):
        pl.semaphore_signal(barrier, inc=1, device_id=(me_s, other), device_id_type=MESH)
    loads[3].start()
    loads[4].start()

    def chip_columns(chip):
        return pl.ds(pl.multiple_of(chip * 2 * lanes, 2 * lanes), 2 * lanes)

    def own_weight(s):
        return pltpu.make_async_copy(
            w_hbm.at[:, chip_columns(chip_at(s))], w_v.at[s, pl.ds(0, features), :], w_sem.at[s]
        )

    def partner_weight(s):
        return pltpu.make_async_remote_copy(
            src_ref=w_hbm.at[:, chip_columns(chip_at(s, 1 - core))],
            dst_ref=w_v.at[s, pl.ds(features, features), :],
            send_sem=w_send.at[s],
            recv_sem=w_recv.at[s],
            device_id=(me_s, partner),
            device_id_type=MESH,
        )

    for s in range(most + 1):
        own_weight(s).start()
    acc[...] = jnp.zeros_like(acc)
    send_acc[...] = jnp.zeros_like(send_acc)

    loads[1].wait()
    decay = dec_v[...]
    pole = jnp.exp(-decay)
    for n in range(orders):
        a_bc[n] = jnp.broadcast_to(pole[n : n + 1], (SUB, lanes))

    zero = jnp.zeros((SUB, lanes), jnp.float32)
    loads[0].wait()
    g_f[...] = g_b[...].astype(jnp.float32)
    unroll = 2

    def gather_states(index, state):
        for inner in range(unroll):
            k = index * unroll + inner
            g_row = g_f[pl.ds(steps - 1 - k, SUB, stride=steps), :]
            state = [g_row + a_bc[n] * state[n] for n in range(orders)]
        return tuple(state)

    ends = lax.fori_loop(0, steps // unroll, gather_states, (zero,) * orders)

    row = lax.broadcasted_iota(jnp.int32, (SUB, lanes), 0)
    for n in range(orders):
        rate = jnp.broadcast_to(dec_v[n : n + 1, :], (SUB, lanes))
        state = ends[n]
        shift = 1
        while shift < SUB:
            moved = jnp.where(row < SUB - shift, pltpu.roll(state, SUB - shift, 0), 0.0)
            state = state + jnp.exp(rate * float(-steps * shift)) * moved
            shift *= 2
        states[me_s, n : n + 1, :] = state[0:1]
        z_bc[n] = jnp.where(row < SUB - 1, pltpu.roll(state, SUB - 1, 0), 0.0)

    pl.semaphore_wait(barrier, me_s + 2)

    def to_peer(buffer, send, recv, hop):
        peer = (me_s + hop) % nseq
        return pltpu.make_async_remote_copy(
            src_ref=buffer.at[me_s],
            dst_ref=buffer.at[me_s],
            send_sem=send.at[hop],
            recv_sem=recv.at[me_s],
            device_id=(peer, me_c),
            device_id_type=MESH,
        )

    def from_peer(buffer, send, recv, hop):
        peer = (me_s + hop) % nseq
        return pltpu.make_async_remote_copy(
            src_ref=buffer.at[peer],
            dst_ref=buffer.at[peer],
            send_sem=send.at[hop],
            recv_sem=recv.at[peer],
            device_id=(peer, me_c),
            device_id_type=MESH,
        )

    for hop in hops:

        @pl.when((me_s + hop) % nseq < me_s)
        def _(hop=hop):
            to_peer(states, st_send, st_recv, hop).start()

    for s in range(most + 1):
        partner_weight(s).start()

    loads[2].wait()
    loads[3].wait()
    loads[4].wait()
    strength = res_v[...] * jnp.sqrt(2.0 * dec_v[...])
    for n in range(orders):
        r_bc[n] = jnp.broadcast_to(strength[n : n + 1], (SUB, lanes))
    act_f[...] = act_b[...].astype(jnp.float32)
    skip_row = jnp.broadcast_to(skip_v[...], (SUB, lanes))
    group = orders // 2
    for part in range(2):
        chosen = range(part * group, (part + 1) * group)
        poles = [a_bc[n] for n in chosen]
        gains = [r_bc[n] for n in chosen]

        def scan(index, carry, poles=poles, gains=gains, part=part):
            state, total = list(carry[0]), list(carry[1])
            for inner in range(unroll):
                k = index * unroll + inner
                g_row = g_f[pl.ds(steps - 1 - k, SUB, stride=steps), :]
                act_row = act_f[pl.ds(steps - 1 - k, SUB, stride=steps), :]
                where = pl.ds(pl.multiple_of(k * SUB, SUB), SUB)
                y = skip_row * g_row if part == 0 else y_f[where, :]
                terms = []
                for m in range(group):
                    state[m] = g_row + poles[m] * state[m]
                    terms.append(gains[m] * state[m])
                    total[m] = total[m] + act_row * state[m]
                while len(terms) > 1:
                    terms = [terms[i] + terms[i + 1] for i in range(0, len(terms), 2)]
                y_f[where, :] = y + terms[0]
            return tuple(state), tuple(total)

        _, total = lax.fori_loop(
            0, steps // unroll, scan, ((zero,) * group, (zero,) * group)
        )
        for m, n in enumerate(chosen):
            l_bc[n] = total[m]

    def weigh(index, carry):
        carry = list(carry)
        for inner in range(unroll):
            j = index * unroll + inner
            act_row = act_f[pl.ds(j, SUB, stride=steps), :]
            for n in range(orders):
                carry[n] = a_bc[n] * (carry[n] + act_row)
        return tuple(carry)

    weights = lax.fori_loop(0, steps // unroll, weigh, (zero,) * orders)
    distance = (SUB - 1 - row).astype(jnp.float32) * float(steps)
    for n in range(orders):
        b_bc[n] = weights[n]
        rate = jnp.broadcast_to(dec_v[n : n + 1, :], (SUB, lanes))
        c_bc[n] = jnp.exp(-rate * distance)
    for later in range(1, nseq):
        blocks = jnp.maximum(later - me_s - 1, 0).astype(jnp.float32) * float(rows)
        e_bc[later] = jnp.where(later > me_s, jnp.exp(dec_v[...] * -blocks), 0.0)

    for hop in hops:

        @pl.when((me_s + hop) % nseq > me_s)
        def _(hop=hop):
            from_peer(states, st_send, st_recv, hop).wait_recv()

    terms = [e_bc[later] * states[later] for later in range(1, nseq)]
    while len(terms) > 1:
        terms = [sum(terms[i : i + 2]) for i in range(0, len(terms), 2)]
    enter = terms[0]
    for n in range(orders):
        c_bc[n] = z_bc[n] + c_bc[n] * jnp.broadcast_to(enter[n : n + 1], (SUB, lanes))

    def rows_of(p):
        return pl.ds(pl.multiple_of(p * piece, piece), piece)

    def pass_on(chip, side, s, p):
        view = gath.at[chip * 2 + side, rows_of(p), :]
        return pltpu.make_async_remote_copy(
            src_ref=view,
            dst_ref=view,
            send_sem=ring_send.at[s, side, p],
            recv_sem=ring_recv.at[s, side, p],
            device_id=(me_s, onward),
            device_id_type=MESH,
        )

    def across(side, p):
        view = gath.at[me_z * 2 + side, rows_of(p), :]
        return pltpu.make_async_remote_copy(
            src_ref=view,
            dst_ref=view,
            send_sem=pr_send.at[p],
            recv_sem=pr_recv.at[p],
            device_id=(me_s, partner),
            device_id_type=MESH,
        )

    def hand_over(p):
        return pltpu.make_async_remote_copy(
            src_ref=send_acc.at[rows_of(p), :],
            dst_ref=inbox.at[rows_of(p), :],
            send_sem=in_send.at[p],
            recv_sem=in_recv.at[p],
            device_id=(me_s, partner),
            device_id_type=MESH,
        )

    poles = [a_bc[n] for n in range(orders)]
    entering = tuple(r_bc[n] * c_bc[n] for n in range(orders))

    def finish(p, carry):
        def pair(index, carry):
            ys = []
            for inner in range(2):
                k = p * (piece // SUB) + index * 2 + inner
                carry = [poles[n] * carry[n] for n in range(orders)]
                terms = list(carry)
                while len(terms) > 1:
                    terms = [terms[i] + terms[i + 1] for i in range(0, len(terms), 2)]
                ys.append(y_f[pl.ds(pl.multiple_of(k * SUB, SUB), SUB), :] + terms[0])
            start = pl.multiple_of(p * piece + index * 2 * SUB, 2 * SUB)
            both = jnp.concatenate(ys, axis=0).astype(jnp.bfloat16)
            gath[me_c, pl.ds(start, 2 * SUB), :] = both
            return tuple(carry)

        carry = lax.fori_loop(0, piece // SUB // 2, pair, carry)
        pass_on(me_z, core, 1, p).start()
        across(core, p).start()
        return carry

    lax.fori_loop(0, PIECES, finish, entering)

    for n in range(orders):
        parts[me_s, n : n + 1, :] = jnp.sum(
            l_bc[n] + b_bc[n] * c_bc[n], axis=0, keepdims=True
        )
    for hop in range(1, nseq):
        to_peer(parts, pt_send, pt_recv, hop).start()

    for p in range(PIECES):
        across(1 - core, p).wait_recv()
        pass_on(me_z, 1 - core, 1, p).start()
    for s in range(most + 1):
        own_weight(s).wait()
        partner_weight(s).wait_recv()

    def multiply(s, p):
        chip = chip_at(s)
        where = rows_of(p)
        block = jnp.concatenate([gath[chip * 2, where, :], gath[chip * 2 + 1, where, :]], axis=1)
        both = lax.dot_general(
            block, w_v[s], (((1,), (1,)), ((), ())), preferred_element_type=jnp.float32
        )
        acc[where, :] += both[:, :features]
        send_acc[where, :] += both[:, features:]

    def ring_step(s, _):
        chip = chip_at(s)
        for turn in range(2):
            side = core if turn == 0 else 1 - core
            for p in range(PIECES):
                pass_on(chip, side, s, p).wait_recv()
                pass_on(chip, side, s + 1, p).start()

                index = turn * PIECES + p
                if index % 2 == 1:
                    u = index // 2

                    @pl.when((s >= 2) | (u // (PIECES // 2) == core))
                    def _(u=u):
                        multiply(s - 1, u)

        return 0

    lax.fori_loop(1, last, ring_step, 0)

    for hop in range(1, nseq):
        from_peer(parts, pt_send, pt_recv, hop).wait_recv()
    total = parts[0]
    for other in range(1, nseq):
        total = total + parts[other]
    rg_ref[...] = total * jnp.sqrt(2.0 * dec_v[...]) * scale_len

    far = chip_at(last)
    for p in range(PIECES):
        pass_on(far, core, last, p).wait_recv()

        @pl.when((last >= 2) | (p // (PIECES // 2) == core))
        def _(p=p):
            multiply(last - 1, p)

    for p in range(PIECES):
        pass_on(far, 1 - core, last, p).wait_recv()
        multiply(last, p)
        hand_over(p).start()

    def deliver(p):
        hand_over(p).wait_recv()
        span = piece // SUB
        for i in range(span):
            k = p * span + i
            where = pl.ds(pl.multiple_of(k * SUB, SUB), SUB)
            nat[pl.ds(steps - 1 - k, SUB, stride=steps), :] = acc[where, :] + inbox[where, :]
        for b in range(SUB):
            where = pl.ds(pl.multiple_of(b * steps + steps - (p + 1) * span, span), span)
            out_ref[where, :] = nat[where, :].astype(out_ref.dtype)

    for p in range(PIECES):
        deliver(p)

    for hop in range(1, nseq):
        to_peer(parts, pt_send, pt_recv, hop).wait_send()

        @pl.when((me_s + hop) % nseq < me_s)
        def _(hop=hop):
            to_peer(states, st_send, st_recv, hop).wait_send()

    for s in range(most + 1):
        partner_weight(s).wait_send()
    for p in range(PIECES):
        across(core, p).wait_send()
        hand_over(p).wait_send()

    def drain(s, _):
        for side in range(2):
            for p in range(PIECES):
                pass_on(me_z, side, s, p).wait_send()
        return 0

    lax.fori_loop(1, last + 1, drain, 0)


def put_out(from_input_grad, from_residue_grad, input_grad, residue_grad, sem):
    copies = [
        pltpu.make_async_copy(from_input_grad, input_grad, sem.at[0]),
        pltpu.make_async_copy(from_residue_grad, residue_grad, sem.at[1]),
    ]
    for copy in copies:
        copy.start()
    for copy in copies:
        copy.wait()


def per_device(nseq, nz, grad_out, activation, residues, decay, skip, in_weight):
    rows, lanes = grad_out.shape
    orders = decay.shape[1]
    features, width = in_weight.shape
    f32, bf16 = jnp.float32, jnp.bfloat16
    ups = reach_up(nz)
    most = max(ups, nz - 1 - ups)
    dma = pltpu.SemaphoreType.DMA
    hbm_spec = pl.BlockSpec(memory_space=pltpu.HBM)
    vmem_spec = pl.BlockSpec(memory_space=pltpu.VMEM)
    spread = pltpu.VMEM((orders, SUB, lanes), f32)
    total = pltpu.VMEM((rows, features), f32)
    arrays = (grad_out, activation, residues.T, decay.T, skip.reshape(1, lanes), in_weight)
    input_grad, residue_grad = pl.pallas_call(
        functools.partial(kernel, nseq, nz, 1.0 / math.sqrt(nseq * rows)),
        out_shape=(
            jax.ShapeDtypeStruct((rows, features), bf16),
            jax.ShapeDtypeStruct((orders, lanes), f32),
        ),
        in_specs=[hbm_spec] * 6,
        out_specs=(vmem_spec, vmem_spec),
        scratch_shapes=[
            pltpu.VMEM((nz * 2, rows, lanes), bf16),
            pltpu.VMEM((most + 1, 2 * features, 2 * lanes), bf16),
            pltpu.VMEM((rows, lanes), bf16),
            pltpu.VMEM((rows, lanes), bf16),
            pltpu.VMEM((orders, lanes), f32),
            pltpu.VMEM((orders, lanes), f32),
            pltpu.VMEM((1, lanes), f32),
            pltpu.VMEM((rows, lanes), f32),
            pltpu.VMEM((rows, lanes), f32),
            pltpu.VMEM((rows, lanes), f32),
            total,
            total,
            total,
            total,
            spread,
            spread,
            spread,
            spread,
            spread,
            spread,
            pltpu.VMEM((nseq, orders, lanes), f32),
            pltpu.VMEM((nseq, orders, lanes), f32),
            pltpu.VMEM((nseq, orders, lanes), f32),
            dma((5,)),
            dma((most + 1,)),
            dma((most + 1,)),
            dma((most + 1,)),
            dma((nseq,)),
            dma((nseq,)),
            dma((nseq,)),
            dma((nseq,)),
            dma((most + 1, 2, PIECES)),
            dma((most + 1, 2, PIECES)),
            dma((PIECES,)),
            dma((PIECES,)),
            dma((PIECES,)),
            dma((PIECES,)),
        ],
        compiler_params=pltpu.CompilerParams(
            collective_id=0, has_side_effects=True, vmem_limit_bytes=40 * 2**20
        ),
        name="modal_backward",
    )(*(pltpu.with_memory_space_constraint(x, pltpu.HBM) for x in arrays))
    input_grad, residue_grad = pl.pallas_call(
        put_out,
        out_shape=(
            jax.ShapeDtypeStruct((rows, features), bf16),
            jax.ShapeDtypeStruct((orders, lanes), f32),
        ),
        in_specs=[vmem_spec, vmem_spec],
        out_specs=(hbm_spec, hbm_spec),
        scratch_shapes=[dma((2,))],
        compiler_params=pltpu.CompilerParams(vmem_limit_bytes=2**20),
        name="put_out",
    )(input_grad, residue_grad)
    return (input_grad, residue_grad.T)


def solution(mesh):
    nseq = mesh.shape["seq"]
    nz = mesh.shape["chan"] // 2
    return jax.shard_map(
        functools.partial(per_device, nseq, nz),
        mesh=mesh,
        in_specs=(
            P("seq", "chan"),
            P("seq", "chan"),
            P("chan", None),
            P("chan", None),
            P("chan"),
            P("chan", None),
        ),
        out_specs=(P("seq", "chan"), P("chan", None)),
        check_vma=False,
    )
```

```python
import functools
import math

import jax
import jax.numpy as jnp
from jax import lax
from jax.experimental import pallas as pl
from jax.experimental.pallas import tpu as pltpu
from jax.sharding import PartitionSpec as P

MESH = pl.DeviceIdType.MESH
SUB = 8
TILT = 0
PIECES = 4


def reach_down(nz):
    return max((nz - 1) // 2 - TILT, 1)


def far_first(nseq):
    edge = max(math.isqrt(nseq), 1)

    def away(hop):
        across, along = divmod(hop, edge)
        return min(across, edge - across) + min(along, edge - along)

    return sorted(range(1, nseq), key=lambda hop: -away(hop))


def kernel(
    nseq,
    nz,
    scale_len,
    g_hbm,
    act_hbm,
    res_hbm,
    dec_hbm,
    skip_hbm,
    w_hbm,
    out_ref,
    rg_ref,
    gath,
    w_v,
    g_b,
    act_b,
    res_v,
    dec_v,
    skip_v,
    g_f,
    act_f,
    y_f,
    acc,
    send_acc,
    inbox,
    nat,
    a_bc,
    r_bc,
    z_bc,
    l_bc,
    b_bc,
    c_bc,
    e_bc,
    states,
    parts,
    load_sem,
    w_sem,
    w_send,
    w_recv,
    st_send,
    st_recv,
    pt_send,
    pt_recv,
    ring_send,
    ring_recv,
    pr_send,
    pr_recv,
    in_send,
    in_recv,
):
    rows, lanes = g_b.shape
    orders = dec_v.shape[0]
    features = w_hbm.shape[0]
    steps = rows // SUB
    downs = reach_down(nz)
    most = max(downs, nz - 1 - downs)
    piece = rows // PIECES
    me_s = lax.axis_index("seq")
    me_c = lax.axis_index("chan")
    me_z = me_c // 2
    core = me_c % 2
    partner = me_z * 2 + (1 - core)
    onward = ((me_z + nz - 1 + 2 * core) % nz) * 2 + core
    source = ((me_z + nz + 1 - 2 * core) % nz) * 2 + core

    last = downs + (nz - 1 - 2 * downs) * core

    def chip_at(s, side=core):
        return (me_z + nz + (1 - 2 * side) * s) % nz

    def load(src, dst, index):
        return pltpu.make_async_copy(src, dst, load_sem.at[index])

    loads = [
        load(g_hbm, g_b, 0),
        load(dec_hbm, dec_v, 1),
        load(res_hbm, res_v, 2),
        load(skip_hbm, skip_v, 3),
        load(act_hbm, act_b, 4),
    ]
    barrier = pltpu.get_barrier_semaphore()
    loads[0].start()
    loads[1].start()
    loads[2].start()
    states[...] = jnp.zeros_like(states)
    hops = far_first(nseq)
    for hop in hops:

        @pl.when((me_s + hop) % nseq > me_s)
        def _(hop=hop):
            pl.semaphore_signal(
                barrier, inc=1, device_id=((me_s + hop) % nseq, me_c), device_id_type=MESH
            )

    for other in (source, partner):
        pl.semaphore_signal(barrier, inc=1, device_id=(me_s, other), device_id_type=MESH)
    loads[3].start()
    loads[4].start()

    def chip_columns(chip):
        return pl.ds(pl.multiple_of(chip * 2 * lanes, 2 * lanes), 2 * lanes)

    def own_weight(s):
        return pltpu.make_async_copy(
            w_hbm.at[:, chip_columns(chip_at(s))], w_v.at[s, pl.ds(0, features), :], w_sem.at[s]
        )

    def partner_weight(s):
        return pltpu.make_async_remote_copy(
            src_ref=w_hbm.at[:, chip_columns(chip_at(s, 1 - core))],
            dst_ref=w_v.at[s, pl.ds(features, features), :],
            send_sem=w_send.at[s],
            recv_sem=w_recv.at[s],
            device_id=(me_s, partner),
            device_id_type=MESH,
        )

    for s in range(most + 1):
        own_weight(s).start()
    acc[...] = jnp.zeros_like(acc)
    send_acc[...] = jnp.zeros_like(send_acc)

    loads[1].wait()
    decay = dec_v[...]
    pole = jnp.exp(-decay)
    for n in range(orders):
        a_bc[n] = jnp.broadcast_to(pole[n : n + 1], (SUB, lanes))

    zero = jnp.zeros((SUB, lanes), jnp.float32)
    loads[0].wait()
    g_f[...] = g_b[...].astype(jnp.float32)
    unroll = 2

    def gather_states(index, state):
        for inner in range(unroll):
            k = index * unroll + inner
            g_row = g_f[pl.ds(steps - 1 - k, SUB, stride=steps), :]
            state = [g_row + a_bc[n] * state[n] for n in range(orders)]
        return tuple(state)

    ends = lax.fori_loop(0, steps // unroll, gather_states, (zero,) * orders)

    row = lax.broadcasted_iota(jnp.int32, (SUB, lanes), 0)
    for n in range(orders):
        rate = jnp.broadcast_to(dec_v[n : n + 1, :], (SUB, lanes))
        state = ends[n]
        shift = 1
        while shift < SUB:
            moved = jnp.where(row < SUB - shift, pltpu.roll(state, SUB - shift, 0), 0.0)
            state = state + jnp.exp(rate * float(-steps * shift)) * moved
            shift *= 2
        states[me_s, n : n + 1, :] = state[0:1]
        z_bc[n] = jnp.where(row < SUB - 1, pltpu.roll(state, SUB - 1, 0), 0.0)

    pl.semaphore_wait(barrier, me_s + 2)

    def to_peer(buffer, send, recv, hop):
        peer = (me_s + hop) % nseq
        return pltpu.make_async_remote_copy(
            src_ref=buffer.at[me_s],
            dst_ref=buffer.at[me_s],
            send_sem=send.at[hop],
            recv_sem=recv.at[me_s],
            device_id=(peer, me_c),
            device_id_type=MESH,
        )

    def from_peer(buffer, send, recv, hop):
        peer = (me_s + hop) % nseq
        return pltpu.make_async_remote_copy(
            src_ref=buffer.at[peer],
            dst_ref=buffer.at[peer],
            send_sem=send.at[hop],
            recv_sem=recv.at[peer],
            device_id=(peer, me_c),
            device_id_type=MESH,
        )

    for hop in hops:

        @pl.when((me_s + hop) % nseq < me_s)
        def _(hop=hop):
            to_peer(states, st_send, st_recv, hop).start()

    for s in range(most + 1):
        partner_weight(s).start()

    loads[2].wait()
    loads[3].wait()
    loads[4].wait()
    strength = res_v[...] * jnp.sqrt(2.0 * dec_v[...])
    for n in range(orders):
        r_bc[n] = jnp.broadcast_to(strength[n : n + 1], (SUB, lanes))
    act_f[...] = act_b[...].astype(jnp.float32)
    skip_row = jnp.broadcast_to(skip_v[...], (SUB, lanes))
    group = orders // 2
    for part in range(2):
        chosen = range(part * group, (part + 1) * group)
        poles = [a_bc[n] for n in chosen]
        gains = [r_bc[n] for n in chosen]

        def scan(index, carry, poles=poles, gains=gains, part=part):
            state, total = list(carry[0]), list(carry[1])
            for inner in range(unroll):
                k = index * unroll + inner
                g_row = g_f[pl.ds(steps - 1 - k, SUB, stride=steps), :]
                act_row = act_f[pl.ds(steps - 1 - k, SUB, stride=steps), :]
                where = pl.ds(pl.multiple_of(k * SUB, SUB), SUB)
                y = skip_row * g_row if part == 0 else y_f[where, :]
                terms = []
                for m in range(group):
                    state[m] = g_row + poles[m] * state[m]
                    terms.append(gains[m] * state[m])
                    total[m] = total[m] + act_row * state[m]
                while len(terms) > 1:
                    terms = [terms[i] + terms[i + 1] for i in range(0, len(terms), 2)]
                y_f[where, :] = y + terms[0]
            return tuple(state), tuple(total)

        _, total = lax.fori_loop(
            0, steps // unroll, scan, ((zero,) * group, (zero,) * group)
        )
        for m, n in enumerate(chosen):
            l_bc[n] = total[m]

    def weigh(index, carry):
        carry = list(carry)
        for inner in range(unroll):
            j = index * unroll + inner
            act_row = act_f[pl.ds(j, SUB, stride=steps), :]
            for n in range(orders):
                carry[n] = a_bc[n] * (carry[n] + act_row)
        return tuple(carry)

    weights = lax.fori_loop(0, steps // unroll, weigh, (zero,) * orders)
    distance = (SUB - 1 - row).astype(jnp.float32) * float(steps)
    for n in range(orders):
        b_bc[n] = weights[n]
        rate = jnp.broadcast_to(dec_v[n : n + 1, :], (SUB, lanes))
        c_bc[n] = jnp.exp(-rate * distance)
    for later in range(1, nseq):
        blocks = jnp.maximum(later - me_s - 1, 0).astype(jnp.float32) * float(rows)
        e_bc[later] = jnp.where(later > me_s, jnp.exp(dec_v[...] * -blocks), 0.0)

    for hop in hops:

        @pl.when((me_s + hop) % nseq > me_s)
        def _(hop=hop):
            from_peer(states, st_send, st_recv, hop).wait_recv()

    terms = [e_bc[later] * states[later] for later in range(1, nseq)]
    while len(terms) > 1:
        terms = [sum(terms[i : i + 2]) for i in range(0, len(terms), 2)]
    enter = terms[0]
    for n in range(orders):
        c_bc[n] = z_bc[n] + c_bc[n] * jnp.broadcast_to(enter[n : n + 1], (SUB, lanes))

    def rows_of(p):
        return pl.ds(pl.multiple_of(p * piece, piece), piece)

    def pass_on(chip, side, s, p):
        view = gath.at[chip * 2 + side, rows_of(p), :]
        return pltpu.make_async_remote_copy(
            src_ref=view,
            dst_ref=view,
            send_sem=ring_send.at[s, side, p],
            recv_sem=ring_recv.at[s, side, p],
            device_id=(me_s, onward),
            device_id_type=MESH,
        )

    def across(side, p):
        view = gath.at[me_z * 2 + side, rows_of(p), :]
        return pltpu.make_async_remote_copy(
            src_ref=view,
            dst_ref=view,
            send_sem=pr_send.at[p],
            recv_sem=pr_recv.at[p],
            device_id=(me_s, partner),
            device_id_type=MESH,
        )

    def hand_over(p):
        return pltpu.make_async_remote_copy(
            src_ref=send_acc.at[rows_of(p), :],
            dst_ref=inbox.at[rows_of(p), :],
            send_sem=in_send.at[p],
            recv_sem=in_recv.at[p],
            device_id=(me_s, partner),
            device_id_type=MESH,
        )

    poles = [a_bc[n] for n in range(orders)]
    entering = tuple(r_bc[n] * c_bc[n] for n in range(orders))

    def finish(p, carry):
        def pair(index, carry):
            ys = []
            for inner in range(2):
                k = p * (piece // SUB) + index * 2 + inner
                carry = [poles[n] * carry[n] for n in range(orders)]
                terms = list(carry)
                while len(terms) > 1:
                    terms = [terms[i] + terms[i + 1] for i in range(0, len(terms), 2)]
                ys.append(y_f[pl.ds(pl.multiple_of(k * SUB, SUB), SUB), :] + terms[0])
            start = pl.multiple_of(p * piece + index * 2 * SUB, 2 * SUB)
            both = jnp.concatenate(ys, axis=0).astype(jnp.bfloat16)
            gath[me_c, pl.ds(start, 2 * SUB), :] = both
            return tuple(carry)

        carry = lax.fori_loop(0, piece // SUB // 2, pair, carry)
        pass_on(me_z, core, 1, p).start()
        across(core, p).start()
        return carry

    lax.fori_loop(0, PIECES, finish, entering)

    for n in range(orders):
        parts[me_s, n : n + 1, :] = jnp.sum(
            l_bc[n] + b_bc[n] * c_bc[n], axis=0, keepdims=True
        )
    for hop in range(1, nseq):
        to_peer(parts, pt_send, pt_recv, hop).start()

    for p in range(PIECES):
        across(1 - core, p).wait_recv()
        pass_on(me_z, 1 - core, 1, p).start()
    for s in range(most + 1):
        own_weight(s).wait()
        partner_weight(s).wait_recv()

    def multiply(s, p):
        chip = chip_at(s)
        where = rows_of(p)
        block = jnp.concatenate([gath[chip * 2, where, :], gath[chip * 2 + 1, where, :]], axis=1)
        both = lax.dot_general(
            block, w_v[s], (((1,), (1,)), ((), ())), preferred_element_type=jnp.float32
        )
        acc[where, :] += both[:, :features]
        send_acc[where, :] += both[:, features:]

    def ring_step(s, _):
        chip = chip_at(s)
        for turn in range(2):
            side = core if turn == 0 else 1 - core
            for p in range(PIECES):
                pass_on(chip, side, s, p).wait_recv()
                pass_on(chip, side, s + 1, p).start()

                index = turn * PIECES + p
                if index % 2 == 1:
                    u = index // 2

                    @pl.when((s >= 2) | (u // (PIECES // 2) == core))
                    def _(u=u):
                        multiply(s - 1, u)

        return 0

    lax.fori_loop(1, last, ring_step, 0)

    for hop in range(1, nseq):
        from_peer(parts, pt_send, pt_recv, hop).wait_recv()
    total = parts[0]
    for other in range(1, nseq):
        total = total + parts[other]
    rg_ref[...] = total * jnp.sqrt(2.0 * dec_v[...]) * scale_len

    far = chip_at(last)
    for p in range(PIECES):
        pass_on(far, core, last, p).wait_recv()

        @pl.when((last >= 2) | (p // (PIECES // 2) == core))
        def _(p=p):
            multiply(last - 1, p)

    for p in range(PIECES):
        pass_on(far, 1 - core, last, p).wait_recv()
        multiply(last, p)
        hand_over(p).start()

    def deliver(p):
        hand_over(p).wait_recv()
        span = piece // SUB
        for i in range(span):
            k = p * span + i
            where = pl.ds(pl.multiple_of(k * SUB, SUB), SUB)
            nat[pl.ds(steps - 1 - k, SUB, stride=steps), :] = acc[where, :] + inbox[where, :]
        for b in range(SUB):
            where = pl.ds(pl.multiple_of(b * steps + steps - (p + 1) * span, span), span)
            out_ref[where, :] = nat[where, :].astype(out_ref.dtype)

    for p in range(PIECES):
        deliver(p)

    for hop in range(1, nseq):
        to_peer(parts, pt_send, pt_recv, hop).wait_send()

        @pl.when((me_s + hop) % nseq < me_s)
        def _(hop=hop):
            to_peer(states, st_send, st_recv, hop).wait_send()

    for s in range(most + 1):
        partner_weight(s).wait_send()
    for p in range(PIECES):
        across(core, p).wait_send()
        hand_over(p).wait_send()

    def drain(s, _):
        for side in range(2):
            for p in range(PIECES):
                pass_on(me_z, side, s, p).wait_send()
        return 0

    lax.fori_loop(1, last + 1, drain, 0)


def put_out(from_input_grad, from_residue_grad, input_grad, residue_grad, sem):
    copies = [
        pltpu.make_async_copy(from_input_grad, input_grad, sem.at[0]),
        pltpu.make_async_copy(from_residue_grad, residue_grad, sem.at[1]),
    ]
    for copy in copies:
        copy.start()
    for copy in copies:
        copy.wait()


def per_device(nseq, nz, grad_out, activation, residues, decay, skip, in_weight):
    rows, lanes = grad_out.shape
    orders = decay.shape[1]
    features, width = in_weight.shape
    f32, bf16 = jnp.float32, jnp.bfloat16
    downs = reach_down(nz)
    most = max(downs, nz - 1 - downs)
    dma = pltpu.SemaphoreType.DMA
    hbm_spec = pl.BlockSpec(memory_space=pltpu.HBM)
    vmem_spec = pl.BlockSpec(memory_space=pltpu.VMEM)
    spread = pltpu.VMEM((orders, SUB, lanes), f32)
    total = pltpu.VMEM((rows, features), f32)
    arrays = (grad_out, activation, residues.T, decay.T, skip.reshape(1, lanes), in_weight)
    input_grad, residue_grad = pl.pallas_call(
        functools.partial(kernel, nseq, nz, 1.0 / math.sqrt(nseq * rows)),
        out_shape=(
            jax.ShapeDtypeStruct((rows, features), bf16),
            jax.ShapeDtypeStruct((orders, lanes), f32),
        ),
        in_specs=[hbm_spec] * 6,
        out_specs=(vmem_spec, vmem_spec),
        scratch_shapes=[
            pltpu.VMEM((nz * 2, rows, lanes), bf16),
            pltpu.VMEM((most + 1, 2 * features, 2 * lanes), bf16),
            pltpu.VMEM((rows, lanes), bf16),
            pltpu.VMEM((rows, lanes), bf16),
            pltpu.VMEM((orders, lanes), f32),
            pltpu.VMEM((orders, lanes), f32),
            pltpu.VMEM((1, lanes), f32),
            pltpu.VMEM((rows, lanes), f32),
            pltpu.VMEM((rows, lanes), f32),
            pltpu.VMEM((rows, lanes), f32),
            total,
            total,
            total,
            total,
            spread,
            spread,
            spread,
            spread,
            spread,
            spread,
            pltpu.VMEM((nseq, orders, lanes), f32),
            pltpu.VMEM((nseq, orders, lanes), f32),
            pltpu.VMEM((nseq, orders, lanes), f32),
            dma((5,)),
            dma((most + 1,)),
            dma((most + 1,)),
            dma((most + 1,)),
            dma((nseq,)),
            dma((nseq,)),
            dma((nseq,)),
            dma((nseq,)),
            dma((most + 1, 2, PIECES)),
            dma((most + 1, 2, PIECES)),
            dma((PIECES,)),
            dma((PIECES,)),
            dma((PIECES,)),
            dma((PIECES,)),
        ],
        compiler_params=pltpu.CompilerParams(
            collective_id=0, has_side_effects=True, vmem_limit_bytes=40 * 2**20
        ),
        name="modal_backward",
    )(*(pltpu.with_memory_space_constraint(x, pltpu.HBM) for x in arrays))
    input_grad, residue_grad = pl.pallas_call(
        put_out,
        out_shape=(
            jax.ShapeDtypeStruct((rows, features), bf16),
            jax.ShapeDtypeStruct((orders, lanes), f32),
        ),
        in_specs=[vmem_spec, vmem_spec],
        out_specs=(hbm_spec, hbm_spec),
        scratch_shapes=[dma((2,))],
        compiler_params=pltpu.CompilerParams(vmem_limit_bytes=2**20),
        name="put_out",
    )(input_grad, residue_grad)
    return (input_grad, residue_grad.T)


def solution(mesh):
    nseq = mesh.shape["seq"]
    nz = mesh.shape["chan"] // 2
    return jax.shard_map(
        functools.partial(per_device, nseq, nz),
        mesh=mesh,
        in_specs=(
            P("seq", "chan"),
            P("seq", "chan"),
            P("chan", None),
            P("chan", None),
            P("chan"),
            P("chan", None),
        ),
        out_specs=(P("seq", "chan"), P("chan", None)),
        check_vma=False,
    )
```
